32 devices in a mesh: section: 2 (over y), expert: 16 (over z, x, core).
Axes of the slice: x: 2, y: 2, z: 4, core: 2. Of those that a mesh axis runs over, the one named last changes fastest.
Arguments:
- x_in: bfloat16 [4, 64, 7168], P(None, 'expert'), may hold values from -6 to 6
- gains: bfloat16 [2, 7168], P('section'), may hold values from 0.25 to 1.75
- router: bfloat16 [2, 7168, 4], P('section'), may hold values from -0.0625 to 0.0625
- w_gate: bfloat16 [2, 16, 2, 7168, 256], P('section', 'expert'), may hold values from -0.0625 to 0.0625
- w_up: bfloat16 [2, 16, 2, 7168, 256], P('section', 'expert'), may hold values from -0.0625 to 0.0625
- w_down: bfloat16 [2, 16, 2, 256, 7168], P('section', 'expert'), may hold values from -0.125 to 0.125
- route_ids: int32 [2, 4, 64, 2], P('section', None, 'expert'), may hold values from 0 to 3, all different within a row; in each aligned block of 4 rows (0 to 3, 4 to 7, ..., all dimensions but the last counted through in order) at most 2 rows name the same one
- stopped: int32 [4, 64], P(None, 'expert'), may hold values 0 or 1
Outputs:
- layer_out: bfloat16 [2, 4, 64, 7168], P('section', None, 'expert')
The draws below stay inside these ranges and needn't reach their ends.
Inputs may be any that keep to these rules, and one draw needn't show every extreme that they name: `route_ids`: each row names 2 different experts. Within one layer and micro-batch, the rows of one device (aligned blocks of 4 rows) name one expert at most 2 times.
All inputs are finite; a program needn't handle non-finite values. No bound on the sum of `stopped` on one device may be relied on, other than what follows from the above.
Results may differ from the reference program's by a relative error of at most 0.019.
Values may be sent and summed in bfloat16 or wider, within the bound.
A program may use at most 128 MiB of HBM per device.

```python
import math
import jax
import jax.numpy as jnp
import numpy as np
from jax import lax

D = 7168
FF = 2048
SHARDS = 8
LOCAL = 2
TOP = 2
MB = 4
ROW_DEV = 4
HID = 256
NE = 4
ROWS = 64
SECTIONS = 2
CAP = 2
N_EXPERT = 16


def touch_ends(entries, rng, smallest, largest):
    extent = entries.shape
    place = [jax.random.randint(jax.random.fold_in(rng, axis), (), 0, extent[axis]) for axis in range(len(extent))]
    entries = entries.at[tuple(place)].set(smallest)
    longest = extent.index(max(extent))
    place[longest] = (place[longest] + 1) % extent[longest]
    return entries.at[tuple(place)].set(largest)


def steps_of(key, extent, pieces, low, top_value):
    level = 1.0
    for axis_at, blocks in pieces:
        steps = jax.random.uniform(jax.random.fold_in(jax.random.fold_in(key, 6), axis_at), (blocks,), jnp.float32, low / len(pieces), top_value / len(pieces))
        level = level * jnp.repeat(jnp.exp(steps), extent[axis_at] // blocks).reshape((-1,) + (1,) * (len(extent) - 1 - axis_at))
    return level


def assign_block(own_key, own, number, rows, number_of, top, most, lean):
    sequence = jax.random.permutation(own_key, number_of)
    heavy_load, usual = load_shares(number_of, rows * top, most, lean, True), load_shares(number_of, rows * top, most, lean, False)
    places = jnp.arange(number_of)

    def named(lengths, turn):
        used = int((lengths > 0).sum())
        fixed = max(1, used // 4)
        passed = fixed + (places - fixed + turn * (used - fixed)) % max(1, number_of - fixed)
        return jnp.zeros((number_of,), jnp.int32).at[sequence[jnp.where(places < fixed, places, passed)]].set(jnp.asarray(lengths, jnp.int32))

    lengths = jnp.where(number % 4 == 0, named(heavy_load, number // 4), named(usual, number - number // 4 - 1))
    mixed = jax.random.permutation(jax.random.fold_in(own, 3), number_of)
    source_of, taker = mixed[0:number_of // 2 * 2:2], mixed[1:number_of // 2 * 2:2]
    room = jnp.minimum(lengths[source_of] - 1, most - lengths[taker]) // 2
    room = jnp.where((source_of == sequence[0]) | (taker == sequence[0]) | (lengths[taker] == 0), 0, jnp.maximum(room, 0))
    passed = jax.random.randint(jax.random.fold_in(own, 4), (number_of // 2,), 0, 1 << 20) % (room + 1)
    lengths = lengths.at[source_of].add(-passed).at[taker].add(passed)
    members = jnp.searchsorted(jnp.cumsum(lengths), jnp.arange(rows * top), side="right").astype(jnp.int32)
    grid = members.reshape(top, rows).T
    grid = grid[jax.random.permutation(jax.random.fold_in(own, 1), rows)]
    turn = jax.random.randint(jax.random.fold_in(own, 2), (rows, 1), 0, top)
    return jnp.take_along_axis(grid, (jnp.arange(top)[None, :] + turn) % top, axis=1)


def load_shares(number_of, total, bound, slope, full):
    weights = [(1 << 20) // math.isqrt(standing ** slope) + 1 for standing in range(1, number_of + 1)]
    largest = bound if full else min(bound, max(-(-total // number_of), total * weights[0] // sum(weights)))
    least = 1 if total - largest >= number_of - 1 else 0
    holding, spare = [largest] + [least] * (number_of - 1), total - largest - least * (number_of - 1)
    while spare > 0:
        movable = [i for i in range(1, number_of) if holding[i] < largest] or [i for i in range(1, number_of) if holding[i] < bound]
        whole, remaining = sum([weights[i] for i in movable]), spare
        for i in movable:
            addition = min(bound - holding[i], max(1, remaining * weights[i] // whole), spare)
            holding[i] = holding[i] + addition
            spare = spare - addition
    return np.array(holding)


def normal_values(own_key, dims, width, most, shards=(), held_as=jnp.bfloat16):
    loudness = steps_of(own_key, dims, shards, -0.22, 0.18) if shards else 1.0
    entries = jax.random.normal(own_key, dims, jnp.float32) * width * loudness
    return jnp.minimum(jnp.maximum(entries, -most), most).astype(held_as)


def setup_inputs(seed: int = 0) -> dict:
    streams_of = jax.random.split(jax.random.key(seed), 9)
    x_in = normal_values(streams_of[0], (MB, ROWS, D), 1.0, 6.0, ((1, 16),))
    gains = jnp.clip(1.0 + 0.15 * jax.random.normal(streams_of[1], (SECTIONS, D), jnp.float32), 0.25, 1.75).astype(jnp.bfloat16)
    router = normal_values(streams_of[2], (SECTIONS, D, NE), D ** -0.5, 0.0625, ((0, 2),))
    w_gate = normal_values(streams_of[3], (SECTIONS, N_EXPERT, LOCAL, D, HID), D ** -0.5, 0.0625, ((0, 2), (1, 16)))
    w_up = normal_values(streams_of[4], (SECTIONS, N_EXPERT, LOCAL, D, HID), D ** -0.5, 0.0625, ((0, 2), (1, 16)))
    w_down = normal_values(streams_of[5], (SECTIONS, N_EXPERT, LOCAL, HID, D), FF ** -0.5, 0.125, ((0, 2), (1, 16)))
    route_ids_keys = jax.random.split(jax.random.fold_in(streams_of[6], 1), SECTIONS * MB * ROWS // ROW_DEV)
    route_ids_turns = jax.random.permutation(jax.random.fold_in(streams_of[6], 3), SECTIONS * MB * ROWS // ROW_DEV)
    route_ids = jax.vmap(lambda own, number: assign_block(jax.random.fold_in(streams_of[6], 2), own, number, ROW_DEV, NE, TOP, CAP, 2))(route_ids_keys, route_ids_turns).reshape((SECTIONS, MB, ROWS, TOP))
    stopped = touch_ends((jax.random.randint(streams_of[7], (MB, ROWS), 0, 4) < 1).astype(jnp.int32), jax.random.fold_in(streams_of[7], 1), 0, 1)
    return dict(x_in=x_in, gains=gains, router=router, w_gate=w_gate, w_up=w_up, w_down=w_down, route_ids=route_ids, stopped=stopped)


def expert_tables(weights):
    shape = weights.shape
    grouped = weights.reshape(NE // LOCAL, SHARDS, LOCAL, shape[-2], shape[-1])
    grouped = jnp.transpose(grouped, (0, 2, 1, 3, 4))
    return grouped.reshape(NE, SHARDS, shape[-2], shape[-1])

def moe_layer(hidden, gain, router_s, gate_tab, up_tab, down_tab, chosen, live):
    widened = hidden.astype(jnp.float32)
    mean_sq = lax.optimization_barrier(jnp.mean(widened * widened, axis=-1, keepdims=True))
    normed = (widened * lax.rsqrt(mean_sq + 1e-06) * gain.astype(jnp.float32)).astype(jnp.bfloat16)
    score = jax.nn.sigmoid(jnp.dot(normed, router_s, preferred_element_type=jnp.float32))
    picked = jnp.take_along_axis(score, chosen, axis=1)
    gates = 2.5 * picked / lax.optimization_barrier(jnp.sum(picked, axis=1, keepdims=True))
    flat_ids = chosen.reshape(-1).astype(jnp.int32)
    flat_live = jnp.repeat(live, TOP)
    sort_key = jnp.where(flat_live > 0, flat_ids, NE).astype(jnp.int32)
    order = jnp.argsort(sort_key, stable=True).astype(jnp.int32)
    sorted_key = sort_key[order]
    span = N_EXPERT * CAP
    order_pad = jnp.concatenate([order, jnp.zeros((span,), jnp.int32)])
    key_pad = jnp.concatenate([sorted_key, jnp.full((span,), NE, jnp.int32)])
    starts = lax.optimization_barrier(jnp.sum((sort_key[None, :] < jnp.arange(NE, dtype=jnp.int32)[:, None]).astype(jnp.int32), axis=1))
    flat_gates = gates.reshape(-1)

    def one_expert(expert):
        begin = starts[expert].astype(jnp.int32)
        index = lax.dynamic_slice(order_pad, (begin,), (span,))
        valid = (lax.dynamic_slice(key_pad, (begin,), (span,)) == expert).astype(jnp.float32)
        rows = normed[index // TOP].astype(jnp.float32)
        gate_w = gate_tab[expert].astype(jnp.float32)
        up_w = up_tab[expert].astype(jnp.float32)
        down_w = down_tab[expert].astype(jnp.float32)
        gate_val = jnp.einsum('md,sdh->smh', rows, gate_w)
        up_val = jnp.einsum('md,sdh->smh', rows, up_w)
        hid = (jax.nn.silu(gate_val) * up_val).astype(jnp.bfloat16)
        part = jnp.einsum('smh,shd->smd', hid.astype(jnp.float32), down_w).astype(jnp.bfloat16)
        summed = lax.optimization_barrier(jnp.sum(part.astype(jnp.float32), axis=0))
        weight = flat_gates[index] * valid
        return (summed * weight[:, None], index // TOP)
    outputs, targets = lax.map(one_expert, jnp.arange(NE, dtype=jnp.int32))
    combined = jnp.zeros((hidden.shape[0], hidden.shape[1]), jnp.float32)
    combined = combined.at[targets.reshape(-1)].add(outputs.reshape(-1, hidden.shape[1]))
    return (widened + combined).astype(jnp.bfloat16)

def reference(x_in, gains, router, w_gate, w_up, w_down, route_ids, stopped):
    per_section = [[None] * MB for section in range(SECTIONS)]
    tables = [(expert_tables(w_gate[section]), expert_tables(w_up[section]), expert_tables(w_down[section])) for section in range(SECTIONS)]
    for batch in range(MB):
        hidden = x_in[batch]
        live = (1 - stopped[batch]).astype(jnp.int32)
        for section in range(SECTIONS):
            gate_tab, up_tab, down_tab = tables[section]
            hidden = moe_layer(hidden, gains[section], router[section], gate_tab, up_tab, down_tab, route_ids[section, batch], live)
            per_section[section][batch] = hidden
    return jnp.stack([jnp.stack(row, axis=0) for row in per_section], axis=0)
```

```python
import functools

import jax
import jax.numpy as jnp
from jax import lax
from jax.experimental import pallas as pl
from jax.experimental.pallas import tpu as pltpu
from jax.sharding import PartitionSpec as P

SHARDS = 8
CHUNKS = 4
MESH = pl.DeviceIdType.MESH
F32 = jnp.float32
BF16 = jnp.bfloat16


def relay_kernel(
    x_ref, gain_ref, router_ref, ids_ref, stop_ref, wg_hbm, wu_hbm, wd_hbm, out_ref,
    hbuf, wg, wu, wd, rows_all, gate_all, acc, hid, part, recv_core, send_x, recv_x, send_a, recv_a,
    w_sem, a_ss, a_rs, x_ss, x_rs, ci_ss, ci_rs, cj_ss, cj_rs,
    r1_ss, r1_rs, r2_ss, r2_rs, r3_ss, r3_rs, h_ss, h_rs,
):
    rows, width = x_ref.shape
    experts = router_ref.shape[0]
    outer = rows_all.shape[2]
    local = wg.shape[0]
    hidden = wg.shape[2]
    cols = width // CHUNKS
    total = 4 * outer * rows
    sections = lax.axis_size("section")
    section = lax.axis_index("section")
    me = lax.axis_index("expert")
    a = me // 4
    b = (me // 2) % 2
    core = me % 2
    twin = a * 4 + b * 2 + (1 - core)
    across = a * 4 + (1 - b) * 2 + core

    def column(step):
        return lax.rem(a + step, outer)

    def at_column(step):
        return column(step) * 4 + b * 2 + core

    loads = [
        pltpu.make_async_copy(wg_hbm, wg, w_sem.at[0]),
        pltpu.make_async_copy(wu_hbm, wu, w_sem.at[1]),
        pltpu.make_async_copy(wd_hbm, wd, w_sem.at[2]),
    ]
    for load in loads:
        load.start()

    barrier = pltpu.get_barrier_semaphore()
    for peer in [at_column(step) for step in range(1, outer)] + [twin, across]:
        pl.semaphore_signal(barrier, inc=1, device_id={"expert": peer}, device_id_type=MESH)

    @pl.when(section > 0)
    def _():
        pl.semaphore_signal(
            barrier, inc=1, device_id={"section": section - 1}, device_id_type=MESH
        )

    @pl.when(section < sections - 1)
    def _():
        pl.semaphore_signal(
            barrier, inc=1, device_id={"section": section + 1}, device_id_type=MESH
        )

    neighbours = jnp.minimum(section, 1) + jnp.minimum(sections - 1 - section, 1)
    pl.semaphore_wait(barrier, outer + 1 + neighbours)

    def span(c):
        return pl.ds(c * cols, cols)

    def remote(src, dst, ss, rs, where):
        return pltpu.make_async_remote_copy(
            src_ref=src, dst_ref=dst, send_sem=ss, recv_sem=rs, device_id=where, device_id_type=MESH
        )

    def h_copy(c):
        return remote(
            out_ref.at[:, span(c)], hbuf.at[:, span(c)], h_ss.at[c], h_rs.at[c],
            {"section": lax.rem(section + 1, sections)},
        )

    @pl.when(section == 0)
    def _():
        hbuf[...] = x_ref[...]

    squares = jnp.zeros((rows, 1), F32)
    for c in range(CHUNKS):
        @pl.when(section > 0)
        def _():
            h_copy(c).wait_recv()

        piece = hbuf[:, span(c)].astype(F32)
        squares = squares + jnp.sum(piece * piece, axis=1, keepdims=True)
    inverse = lax.rsqrt(squares / width + 1e-06)

    def gather_refs(c, *index):
        if c == CHUNKS:
            return gate_all.at[index]
        return rows_all.at[index + (slice(None),) * (4 - len(index)) + (span(c),)]

    def a_copy(c, step):
        here = gather_refs(c, core, b, a)
        return remote(
            here, here, a_ss.at[c, step - 1], a_rs.at[c, step - 1], {"expert": at_column(step)}
        )

    def x_copy(c):
        here = gather_refs(c, core, b)
        return remote(here, here, x_ss.at[c], x_rs.at[c], {"expert": across})

    def ci_copy(c):
        here = gather_refs(c, core, b)
        return remote(here, here, ci_ss.at[c], ci_rs.at[c], {"expert": twin})

    def cj_copy(c):
        here = gather_refs(c, core, 1 - b)
        return remote(here, here, cj_ss.at[c], cj_rs.at[c], {"expert": twin})

    logits = [jnp.zeros((rows, 1), F32) for _ in range(experts)]
    for c in range(CHUNKS):
        piece = hbuf[:, span(c)].astype(F32)
        normed = (piece * inverse * gain_ref[:, span(c)].astype(F32)).astype(BF16)
        rows_all[core, b, a, :, span(c)] = normed
        for step in range(1, outer):
            a_copy(c, step).start()
        wide = normed.astype(F32)
        for e in range(experts):
            logits[e] = logits[e] + jnp.sum(
                wide * router_ref[e : e + 1, span(c)].astype(F32), axis=1, keepdims=True
            )

    ids = ids_ref[...]
    live = stop_ref[...] == 0
    scores = [jax.nn.sigmoid(value) for value in logits]
    chosen = [(ids[:, 0:1] == e) | (ids[:, 1:2] == e) for e in range(experts)]
    norm = jnp.zeros((rows, 1), F32)
    for e in range(experts):
        norm = norm + jnp.where(chosen[e], scores[e], 0.0)
    lanes = lax.broadcasted_iota(jnp.int32, (rows, 128), 1)
    gates = jnp.zeros((rows, 128), F32)
    for e in range(experts):
        value = jnp.where(chosen[e] & live, 2.5 * scores[e] / norm, 0.0)
        gates = gates + jnp.where(lanes == e, value, 0.0)
    gate_all[core, b, a] = gates
    for step in range(1, outer):
        a_copy(CHUNKS, step).start()

    order = list(range(CHUNKS)) + [CHUNKS]

    def stage_a(c):
        for step in range(1, outer):
            a_copy(c, step).wait_recv()
        x_copy(c).start()
        ci_copy(c).start()

    def stage_x(c):
        x_copy(c).wait_recv()
        cj_copy(c).start()

    def multiply(c):
        ci_copy(c).wait_recv()
        cj_copy(c).wait_recv()
        if c == CHUNKS:
            return
        if c == 0:
            loads[0].wait()
            loads[1].wait()
        block = rows_all[:, :, :, :, span(c)].reshape(total, cols)
        for k in range(local):
            for i, w in enumerate((wg, wu)):
                product = jnp.dot(block, w[k, span(c), :], preferred_element_type=F32)
                if c == 0:
                    acc[k, i] = product
                else:
                    acc[k, i] = acc[k, i] + product

    count = len(order)
    for t in range(count + 2):
        if t < count:
            stage_a(order[t])
        if 1 <= t < count + 1:
            stage_x(order[t - 1])
        if t >= 2:
            multiply(order[t - 2])

    weights = gate_all[...].reshape(total, 128)
    lanes_all = lax.broadcasted_iota(jnp.int32, (total, 128), 1)
    for k in range(local):
        expert = local * (me // SHARDS) + k
        weight = jnp.sum(jnp.where(lanes_all == expert, weights, 0.0), axis=1, keepdims=True)
        value = acc[k, 0]
        value = value / (1.0 + jnp.exp(-value)) * acc[k, 1]
        hid[:, k * hidden : (k + 1) * hidden] = jnp.where(
            weight != 0.0, value * weight, 0.0
        ).astype(BF16)

    loads[2].wait()

    def r1_copy(c):
        return remote(
            part.at[1 - core, :, :, :, span(c)], recv_core.at[:, :, :, span(c)],
            r1_ss.at[c], r1_rs.at[c], {"expert": twin},
        )

    def r2_copy(c):
        return remote(
            send_x.at[:, :, span(c)], recv_x.at[:, :, span(c)],
            r2_ss.at[c], r2_rs.at[c], {"expert": across},
        )

    def r3_copy(c, step):
        return remote(
            send_a.at[step - 1, :, span(c)], recv_a.at[step - 1, :, span(c)],
            r3_ss.at[c, step - 1], r3_rs.at[c, step - 1], {"expert": at_column(step)},
        )

    tile = 256

    def down(c):
        @pl.loop(0, cols // tile)
        def _(j):
            at = pl.ds(pl.multiple_of(c * cols + j * tile, tile), tile)
            product = jnp.dot(hid[...], wd[:, at], preferred_element_type=F32)
            part[:, :, :, :, at] = product.astype(BF16).reshape(2, 2, outer, rows, tile)

        r1_copy(c).start()

    def add_core(c):
        r1_copy(c).wait_recv()
        for i in range(outer):
            send_x[i, :, span(c)] = (
                part[core, 1 - b, i, :, span(c)].astype(F32)
                + recv_core[1 - b, i, :, span(c)].astype(F32)
            ).astype(BF16)
        r2_copy(c).start()

    def column_sum(c, i):
        return (
            part[core, b, i, :, span(c)].astype(F32)
            + recv_core[b, i, :, span(c)].astype(F32)
            + recv_x[i, :, span(c)].astype(F32)
        )

    def add_x(c):
        r2_copy(c).wait_recv()
        for step in range(1, outer):
            send_a[step - 1, :, span(c)] = column_sum(c, column(step)).astype(BF16)
            r3_copy(c, step).start()

    def finish(c):
        result = column_sum(c, a)
        for step in range(1, outer):
            r3_copy(c, step).wait_recv()
            result = result + recv_a[step - 1, :, span(c)].astype(F32)
        out_ref[:, span(c)] = (hbuf[:, span(c)].astype(F32) + result).astype(BF16)

        @pl.when(section < sections - 1)
        def _():
            h_copy(c).start()

    for t in range(CHUNKS + 3):
        if t < CHUNKS:
            down(t)
        if 1 <= t < CHUNKS + 1:
            add_core(t - 1)
        if 2 <= t < CHUNKS + 2:
            add_x(t - 2)
        if t >= 3:
            finish(t - 3)

    for c in order:
        for step in range(1, outer):
            a_copy(c, step).wait_send()
        x_copy(c).wait_send()
        ci_copy(c).wait_send()
        cj_copy(c).wait_send()
    for c in range(CHUNKS):
        r1_copy(c).wait_send()
        r2_copy(c).wait_send()
        for step in range(1, outer):
            r3_copy(c, step).wait_send()

    @pl.when(section < sections - 1)
    def _():
        for c in range(CHUNKS):
            h_copy(c).wait_send()


def shards(x_in, gains, router, w_gate, w_up, w_down, route_ids, stopped):
    batches, per, width = x_in.shape
    rows = batches * per
    local, _, hidden = w_gate.shape[2:]
    experts = router.shape[2]
    picks = route_ids.shape[3]
    outer = lax.axis_size("expert") // 4
    dma = lambda *shape: pltpu.SemaphoreType.DMA(shape)
    vmem = pl.BlockSpec(memory_space=pltpu.VMEM)
    anywhere = pl.BlockSpec(memory_space=pl.ANY)
    total = 4 * outer * rows
    more = CHUNKS + 1
    result = pl.pallas_call(
        relay_kernel,
        out_shape=jax.ShapeDtypeStruct((rows, width), BF16),
        in_specs=[vmem] * 5 + [anywhere] * 3,
        out_specs=vmem,
        scratch_shapes=[
            pltpu.VMEM((rows, width), BF16),
            pltpu.VMEM((local, width, hidden), BF16),
            pltpu.VMEM((local, width, hidden), BF16),
            pltpu.VMEM((local * hidden, width), BF16),
            pltpu.VMEM((2, 2, outer, rows, width), BF16),
            pltpu.VMEM((2, 2, outer, rows, 128), F32),
            pltpu.VMEM((local, 2, total, hidden), F32),
            pltpu.VMEM((total, local * hidden), BF16),
            pltpu.VMEM((2, 2, outer, rows, width), BF16),
            pltpu.VMEM((2, outer, rows, width), BF16),
            pltpu.VMEM((outer, rows, width), BF16),
            pltpu.VMEM((outer, rows, width), BF16),
            pltpu.VMEM((outer - 1, rows, width), BF16),
            pltpu.VMEM((outer - 1, rows, width), BF16),
            dma(3),
            dma(more, outer - 1), dma(more, outer - 1),
            dma(more), dma(more), dma(more), dma(more), dma(more), dma(more),
            dma(CHUNKS), dma(CHUNKS), dma(CHUNKS), dma(CHUNKS),
            dma(CHUNKS, outer - 1), dma(CHUNKS, outer - 1),
            dma(CHUNKS), dma(CHUNKS),
        ],
        compiler_params=pltpu.CompilerParams(
            collective_id=0, has_side_effects=True, vmem_limit_bytes=66 * 1000 * 1000
        ),
    )(
        x_in.reshape(rows, width),
        gains,
        jnp.transpose(router[0]),
        route_ids.reshape(rows, picks),
        stopped.reshape(rows, 1),
        w_gate[0, 0],
        w_up[0, 0],
        w_down.reshape(local * hidden, width),
    )
    return result.reshape(1, batches, per, width)


def solution(mesh):
    in_specs = (
        P(None, "expert", None),
        P("section", None),
        P("section", None, None),
        P("section", "expert", None, None, None),
        P("section", "expert", None, None, None),
        P("section", "expert", None, None, None),
        P("section", None, "expert", None),
        P(None, "expert"),
    )
    out_specs = P("section", None, "expert", None)
    return jax.shard_map(shards, mesh=mesh, in_specs=in_specs, out_specs=out_specs, check_vma=False)
```

```python
import functools

import jax
import jax.numpy as jnp
from jax import lax
from jax.experimental import pallas as pl
from jax.experimental.pallas import tpu as pltpu
from jax.sharding import PartitionSpec as P

SHARDS = 8
CHUNKS = 4
PARTS = 2
MESH = pl.DeviceIdType.MESH
F32 = jnp.float32
BF16 = jnp.bfloat16


def relay_kernel(
    x_ref, gain_ref, router_ref, ids_ref, stop_ref, wg_hbm, wu_hbm, wd_hbm, out_ref,
    hbuf, wg, wu, wd, rows_all, gate_all, acc, hid, part, recv_core, send_x, recv_x, send_a, recv_a,
    w_sem, a_ss, a_rs, x_ss, x_rs, ci_ss, ci_rs, cj_ss, cj_rs,
    r1_ss, r1_rs, r2_ss, r2_rs, r3_ss, r3_rs, h_ss, h_rs,
):
    _, rows, width = x_ref.shape
    experts = router_ref.shape[0]
    outer = rows_all.shape[3]
    local = wg.shape[0]
    hidden = wg.shape[2]
    cols = width // CHUNKS
    total = 4 * outer * rows
    sections = lax.axis_size("section")
    section = lax.axis_index("section")
    me = lax.axis_index("expert")
    a = me // 4
    b = (me // 2) % 2
    core = me % 2
    twin = a * 4 + b * 2 + (1 - core)
    across = a * 4 + (1 - b) * 2 + core

    def column(step):
        return lax.rem(a + step, outer)

    def at_column(step):
        return column(step) * 4 + b * 2 + core

    loads = [
        pltpu.make_async_copy(wg_hbm, wg, w_sem.at[0]),
        pltpu.make_async_copy(wu_hbm, wu, w_sem.at[1]),
        pltpu.make_async_copy(wd_hbm, wd, w_sem.at[2]),
    ]
    for load in loads:
        load.start()

    barrier = pltpu.get_barrier_semaphore()
    for peer in [at_column(step) for step in range(1, outer)] + [twin, across]:
        pl.semaphore_signal(barrier, inc=1, device_id={"expert": peer}, device_id_type=MESH)

    @pl.when(section > 0)
    def _():
        pl.semaphore_signal(
            barrier, inc=1, device_id={"section": section - 1}, device_id_type=MESH
        )

    @pl.when(section < sections - 1)
    def _():
        pl.semaphore_signal(
            barrier, inc=1, device_id={"section": section + 1}, device_id_type=MESH
        )

    neighbours = jnp.minimum(section, 1) + jnp.minimum(sections - 1 - section, 1)
    pl.semaphore_wait(barrier, outer + 1 + neighbours)

    def span(c):
        return pl.ds(c * cols, cols)

    def remote(src, dst, ss, rs, where):
        return pltpu.make_async_remote_copy(
            src_ref=src, dst_ref=dst, send_sem=ss, recv_sem=rs, device_id=where, device_id_type=MESH
        )

    def h_copy(p, c):
        return remote(
            out_ref.at[p, :, span(c)], hbuf.at[p, :, span(c)], h_ss.at[p, c], h_rs.at[p, c],
            {"section": lax.rem(section + 1, sections)},
        )

    @pl.when(section == 0)
    def _():
        hbuf[...] = x_ref[...]

    def gather_refs(p, c, *index):
        if c == CHUNKS:
            return gate_all.at[(p,) + index]
        return rows_all.at[(p,) + index + (slice(None),) * (4 - len(index)) + (span(c),)]

    def a_copy(p, c, step):
        here = gather_refs(p, c, core, b, a)
        return remote(
            here, here, a_ss.at[p, c, step - 1], a_rs.at[p, c, step - 1],
            {"expert": at_column(step)},
        )

    def x_copy(p, c):
        here = gather_refs(p, c, core, b)
        return remote(here, here, x_ss.at[p, c], x_rs.at[p, c], {"expert": across})

    def ci_copy(p, c):
        here = gather_refs(p, c, core, b)
        return remote(here, here, ci_ss.at[p, c], ci_rs.at[p, c], {"expert": twin})

    def cj_copy(p, c):
        here = gather_refs(p, c, core, 1 - b)
        return remote(here, here, cj_ss.at[p, c], cj_rs.at[p, c], {"expert": twin})

    def send_rows(p, waits):
        squares = jnp.zeros((rows, 1), F32)
        for c in range(CHUNKS):
            if waits:
                h_copy(p, c).wait_recv()
            piece = hbuf[p, :, span(c)].astype(F32)
            squares = squares + jnp.sum(piece * piece, axis=1, keepdims=True)
        inverse = lax.rsqrt(squares / width + 1e-06)
        logits = [jnp.zeros((rows, 1), F32) for _ in range(experts)]
        for c in range(CHUNKS):
            piece = hbuf[p, :, span(c)].astype(F32)
            normed = (piece * inverse * gain_ref[:, span(c)].astype(F32)).astype(BF16)
            rows_all[p, core, b, a, :, span(c)] = normed
            for step in range(1, outer):
                a_copy(p, c, step).start()
            wide = normed.astype(F32)
            for e in range(experts):
                logits[e] = logits[e] + jnp.sum(
                    wide * router_ref[e : e + 1, span(c)].astype(F32), axis=1, keepdims=True
                )
        ids = ids_ref[p]
        live = stop_ref[p] == 0
        scores = [jax.nn.sigmoid(value) for value in logits]
        chosen = [(ids[:, 0:1] == e) | (ids[:, 1:2] == e) for e in range(experts)]
        norm = jnp.zeros((rows, 1), F32)
        for e in range(experts):
            norm = norm + jnp.where(chosen[e], scores[e], 0.0)
        lanes = lax.broadcasted_iota(jnp.int32, (rows, 128), 1)
        gates = jnp.zeros((rows, 128), F32)
        for e in range(experts):
            value = jnp.where(chosen[e] & live, 2.5 * scores[e] / norm, 0.0)
            gates = gates + jnp.where(lanes == e, value, 0.0)
        gate_all[p, core, b, a] = gates
        for step in range(1, outer):
            a_copy(p, CHUNKS, step).start()

    def stage_a(p, c):
        for step in range(1, outer):
            a_copy(p, c, step).wait_recv()
        x_copy(p, c).start()
        ci_copy(p, c).start()

    def stage_x(p, c):
        x_copy(p, c).wait_recv()
        cj_copy(p, c).start()

    def multiply(p, c):
        ci_copy(p, c).wait_recv()
        cj_copy(p, c).wait_recv()
        if c == CHUNKS:
            return
        if c == 0 and p == 0:
            loads[0].wait()
            loads[1].wait()
        block = rows_all[p, :, :, :, :, span(c)].reshape(total, cols)
        for k in range(local):
            for i, w in enumerate((wg, wu)):
                product = jnp.dot(block, w[k, span(c), :], preferred_element_type=F32)
                if c == 0:
                    acc[k, i] = product
                else:
                    acc[k, i] = acc[k, i] + product

    def activate(p):
        weights = gate_all[p].reshape(total, 128)
        lanes_all = lax.broadcasted_iota(jnp.int32, (total, 128), 1)
        for k in range(local):
            expert = local * (me // SHARDS) + k
            weight = jnp.sum(jnp.where(lanes_all == expert, weights, 0.0), axis=1, keepdims=True)
            value = acc[k, 0]
            value = value / (1.0 + jnp.exp(-value)) * acc[k, 1]
            hid[:, k * hidden : (k + 1) * hidden] = jnp.where(
                weight != 0.0, value * weight, 0.0
            ).astype(BF16)

    def r1_copy(p, c):
        return remote(
            part.at[p, 1 - core, :, :, :, span(c)], recv_core.at[p, :, :, :, span(c)],
            r1_ss.at[p, c], r1_rs.at[p, c], {"expert": twin},
        )

    def r2_copy(p, c):
        return remote(
            send_x.at[p, :, :, span(c)], recv_x.at[p, :, :, span(c)],
            r2_ss.at[p, c], r2_rs.at[p, c], {"expert": across},
        )

    def r3_copy(p, c, step):
        return remote(
            send_a.at[p, step - 1, :, span(c)], recv_a.at[p, step - 1, :, span(c)],
            r3_ss.at[p, c, step - 1], r3_rs.at[p, c, step - 1], {"expert": at_column(step)},
        )

    tile = 256

    def down(p, c):
        if c == 0 and p == 0:
            loads[2].wait()

        @pl.loop(0, cols // tile)
        def _(j):
            at = pl.ds(pl.multiple_of(c * cols + j * tile, tile), tile)
            product = jnp.dot(hid[...], wd[:, at], preferred_element_type=F32)
            part[p, :, :, :, :, at] = product.reshape(2, 2, outer, rows, tile).astype(BF16)

        r1_copy(p, c).start()

    def add_core(p, c):
        r1_copy(p, c).wait_recv()
        for i in range(outer):
            send_x[p, i, :, span(c)] = (
                part[p, core, 1 - b, i, :, span(c)].astype(F32)
                + recv_core[p, 1 - b, i, :, span(c)].astype(F32)
            ).astype(BF16)
        r2_copy(p, c).start()

    def column_sum(p, c, i):
        return (
            part[p, core, b, i, :, span(c)].astype(F32)
            + recv_core[p, b, i, :, span(c)].astype(F32)
            + recv_x[p, i, :, span(c)].astype(F32)
        )

    def add_x(p, c):
        r2_copy(p, c).wait_recv()
        for step in range(1, outer):
            send_a[p, step - 1, :, span(c)] = column_sum(p, c, column(step)).astype(BF16)
            r3_copy(p, c, step).start()

    def finish(p, c):
        result = column_sum(p, c, a)
        for step in range(1, outer):
            r3_copy(p, c, step).wait_recv()
            result = result + recv_a[p, step - 1, :, span(c)].astype(F32)
        out_ref[p, :, span(c)] = (hbuf[p, :, span(c)].astype(F32) + result).astype(BF16)

        @pl.when(section < sections - 1)
        def _():
            h_copy(p, c).start()

    everything = CHUNKS + 1

    @pl.when(section == 0)
    def _():
        for p in range(PARTS):
            send_rows(p, False)

    @pl.when(section > 0)
    def _():
        send_rows(0, True)

    for p in range(PARTS + 1):
        for t in range(CHUNKS + 4):
            if p > 0 and t < CHUNKS:
                down(p - 1, t)
            if p < PARTS and t < everything:
                stage_a(p, t)
            if p > 0 and 1 <= t < CHUNKS + 1:
                add_core(p - 1, t - 1)
            if p < PARTS and 1 <= t < everything + 1:
                stage_x(p, t - 1)
            if p > 0 and 2 <= t < CHUNKS + 2:
                add_x(p - 1, t - 2)
            if p + 1 < PARTS and t == everything:

                @pl.when(section > 0)
                def _():
                    send_rows(p + 1, True)

            if p < PARTS and 2 <= t < everything + 2:
                multiply(p, t - 2)
            if p > 0 and 3 <= t < CHUNKS + 3:
                finish(p - 1, t - 3)
        if p < PARTS:
            activate(p)

    for p in range(PARTS):
        for c in range(everything):
            for step in range(1, outer):
                a_copy(p, c, step).wait_send()
            x_copy(p, c).wait_send()
            ci_copy(p, c).wait_send()
            cj_copy(p, c).wait_send()
        for c in range(CHUNKS):
            r1_copy(p, c).wait_send()
            r2_copy(p, c).wait_send()
            for step in range(1, outer):
                r3_copy(p, c, step).wait_send()

    @pl.when(section < sections - 1)
    def _():
        for p in range(PARTS):
            for c in range(CHUNKS):
                h_copy(p, c).wait_send()


def shards(x_in, gains, router, w_gate, w_up, w_down, route_ids, stopped):
    batches, per, width = x_in.shape
    rows = batches * per // PARTS
    local, _, hidden = w_gate.shape[2:]
    experts = router.shape[2]
    picks = route_ids.shape[3]
    outer = lax.axis_size("expert") // 4
    dma = lambda *shape: pltpu.SemaphoreType.DMA(shape)
    vmem = pl.BlockSpec(memory_space=pltpu.VMEM)
    anywhere = pl.BlockSpec(memory_space=pl.ANY)
    total = 4 * outer * rows
    more = CHUNKS + 1
    result = pl.pallas_call(
        relay_kernel,
        out_shape=jax.ShapeDtypeStruct((PARTS, rows, width), BF16),
        in_specs=[vmem] * 5 + [anywhere] * 3,
        out_specs=vmem,
        scratch_shapes=[
            pltpu.VMEM((PARTS, rows, width), BF16),
            pltpu.VMEM((local, width, hidden), BF16),
            pltpu.VMEM((local, width, hidden), BF16),
            pltpu.VMEM((local * hidden, width), BF16),
            pltpu.VMEM((PARTS, 2, 2, outer, rows, width), BF16),
            pltpu.VMEM((PARTS, 2, 2, outer, rows, 128), F32),
            pltpu.VMEM((local, 2, total, hidden), F32),
            pltpu.VMEM((total, local * hidden), BF16),
            pltpu.VMEM((PARTS, 2, 2, outer, rows, width), BF16),
            pltpu.VMEM((PARTS, 2, outer, rows, width), BF16),
            pltpu.VMEM((PARTS, outer, rows, width), BF16),
            pltpu.VMEM((PARTS, outer, rows, width), BF16),
            pltpu.VMEM((PARTS, outer - 1, rows, width), BF16),
            pltpu.VMEM((PARTS, outer - 1, rows, width), BF16),
            dma(3),
            dma(PARTS, more, outer - 1), dma(PARTS, more, outer - 1),
            dma(PARTS, more), dma(PARTS, more), dma(PARTS, more), dma(PARTS, more), dma(PARTS, more), dma(PARTS, more),
            dma(PARTS, CHUNKS), dma(PARTS, CHUNKS), dma(PARTS, CHUNKS), dma(PARTS, CHUNKS),
            dma(PARTS, CHUNKS, outer - 1), dma(PARTS, CHUNKS, outer - 1),
            dma(PARTS, CHUNKS), dma(PARTS, CHUNKS),
        ],
        compiler_params=pltpu.CompilerParams(
            collective_id=0, has_side_effects=True, vmem_limit_bytes=66 * 1000 * 1000
        ),
    )(
        x_in.reshape(PARTS, rows, width),
        gains,
        jnp.transpose(router[0]),
        route_ids.reshape(PARTS, rows, picks),
        stopped.reshape(PARTS, rows, 1),
        w_gate[0, 0],
        w_up[0, 0],
        w_down.reshape(local * hidden, width),
    )
    return result.reshape(1, batches, per, width)


def solution(mesh):
    in_specs = (
        P(None, "expert", None),
        P("section", None),
        P("section", None, None),
        P("section", "expert", None, None, None),
        P("section", "expert", None, None, None),
        P("section", "expert", None, None, None),
        P("section", None, "expert", None),
        P(None, "expert"),
    )
    out_specs = P("section", None, "expert", None)
    return jax.shard_map(shards, mesh=mesh, in_specs=in_specs, out_specs=out_specs, check_vma=False)
```

```python
import functools

import jax
import jax.numpy as jnp
from jax import lax
from jax.experimental import pallas as pl
from jax.experimental.pallas import tpu as pltpu
from jax.sharding import PartitionSpec as P

SHARDS = 8
CHUNKS = 7
PARTS = 2
GATHER_LAGS = (2, 3)
REDUCE_LAGS = (1, 3, 5)
MESH = pl.DeviceIdType.MESH
F32 = jnp.float32
BF16 = jnp.bfloat16


def relay_kernel(
    x_ref, gain_ref, router_ref, ids_ref, stop_ref, wg_hbm, wu_hbm, wd_hbm, out_ref,
    hbuf, wg, wu, wd, rows_all, gate_all, acc, hid, part, recv_core, send_x, recv_x, send_a, recv_a,
    w_sem, a_ss, a_rs, x_ss, x_rs, ci_ss, ci_rs, cj_ss, cj_rs,
    r1_ss, r1_rs, r2_ss, r2_rs, r3_ss, r3_rs, h_ss, h_rs,
):
    _, rows, width = x_ref.shape
    experts = router_ref.shape[0]
    outer = rows_all.shape[3]
    local = wg.shape[0]
    hidden = wg.shape[2]
    cols = width // CHUNKS
    total = 4 * outer * rows
    sections = lax.axis_size("section")
    section = lax.axis_index("section")
    me = lax.axis_index("expert")
    a = me // 4
    b = (me // 2) % 2
    core = me % 2
    twin = a * 4 + b * 2 + (1 - core)
    across = a * 4 + (1 - b) * 2 + core

    def column(step):
        return lax.rem(a + step, outer)

    def at_column(step):
        return column(step) * 4 + b * 2 + core

    loads = [
        pltpu.make_async_copy(wg_hbm, wg, w_sem.at[0]),
        pltpu.make_async_copy(wu_hbm, wu, w_sem.at[1]),
        pltpu.make_async_copy(wd_hbm, wd, w_sem.at[2]),
    ]
    for load in loads:
        load.start()

    barrier = pltpu.get_barrier_semaphore()
    for peer in [at_column(step) for step in range(1, outer)] + [twin, across]:
        pl.semaphore_signal(barrier, inc=1, device_id={"expert": peer}, device_id_type=MESH)

    @pl.when(section > 0)
    def _():
        pl.semaphore_signal(
            barrier, inc=1, device_id={"section": section - 1}, device_id_type=MESH
        )

    @pl.when(section < sections - 1)
    def _():
        pl.semaphore_signal(
            barrier, inc=1, device_id={"section": section + 1}, device_id_type=MESH
        )

    neighbours = jnp.minimum(section, 1) + jnp.minimum(sections - 1 - section, 1)
    pl.semaphore_wait(barrier, outer + 1 + neighbours)

    def span(c):
        return pl.ds(c * cols, cols)

    def remote(src, dst, ss, rs, where):
        return pltpu.make_async_remote_copy(
            src_ref=src, dst_ref=dst, send_sem=ss, recv_sem=rs, device_id=where, device_id_type=MESH
        )

    def h_copy(p, c):
        return remote(
            out_ref.at[p, :, span(c)], hbuf.at[p, :, span(c)], h_ss.at[p, c], h_rs.at[p, c],
            {"section": lax.rem(section + 1, sections)},
        )

    @pl.when(section == 0)
    def _():
        hbuf[...] = x_ref[...]

    def gather_refs(p, c, *index):
        if c == CHUNKS:
            return gate_all.at[(p,) + index]
        return rows_all.at[(p,) + index + (slice(None),) * (4 - len(index)) + (span(c),)]

    def a_copy(p, c, step):
        here = gather_refs(p, c, core, b, a)
        return remote(
            here, here, a_ss.at[p, c, step - 1], a_rs.at[p, c, step - 1],
            {"expert": at_column(step)},
        )

    def x_copy(p, c):
        here = gather_refs(p, c, core, b)
        return remote(here, here, x_ss.at[p, c], x_rs.at[p, c], {"expert": across})

    def ci_copy(p, c):
        here = gather_refs(p, c, core, b)
        return remote(here, here, ci_ss.at[p, c], ci_rs.at[p, c], {"expert": twin})

    def cj_copy(p, c):
        here = gather_refs(p, c, core, 1 - b)
        return remote(here, here, cj_ss.at[p, c], cj_rs.at[p, c], {"expert": twin})

    def send_rows(p, waits):
        squares = jnp.zeros((rows, 1), F32)
        for c in range(CHUNKS):
            if waits:
                h_copy(p, c).wait_recv()
            piece = hbuf[p, :, span(c)].astype(F32)
            squares = squares + jnp.sum(piece * piece, axis=1, keepdims=True)
        inverse = lax.rsqrt(squares / width + 1e-06)
        logits = [jnp.zeros((rows, 1), F32) for _ in range(experts)]
        for c in range(CHUNKS):
            piece = hbuf[p, :, span(c)].astype(F32)
            normed = (piece * inverse * gain_ref[:, span(c)].astype(F32)).astype(BF16)
            rows_all[p, core, b, a, :, span(c)] = normed
            for step in range(1, outer):
                a_copy(p, c, step).start()
            wide = normed.astype(F32)
            for e in range(experts):
                logits[e] = logits[e] + jnp.sum(
                    wide * router_ref[e : e + 1, span(c)].astype(F32), axis=1, keepdims=True
                )
        ids = ids_ref[p]
        live = stop_ref[p] == 0
        scores = [jax.nn.sigmoid(value) for value in logits]
        chosen = [(ids[:, 0:1] == e) | (ids[:, 1:2] == e) for e in range(experts)]
        norm = jnp.zeros((rows, 1), F32)
        for e in range(experts):
            norm = norm + jnp.where(chosen[e], scores[e], 0.0)
        lanes = lax.broadcasted_iota(jnp.int32, (rows, 128), 1)
        gates = jnp.zeros((rows, 128), F32)
        for e in range(experts):
            value = jnp.where(chosen[e] & live, 2.5 * scores[e] / norm, 0.0)
            gates = gates + jnp.where(lanes == e, value, 0.0)
        gate_all[p, core, b, a] = gates
        for step in range(1, outer):
            a_copy(p, CHUNKS, step).start()

    def stage_a(p, c):
        for step in range(1, outer):
            a_copy(p, c, step).wait_recv()
        x_copy(p, c).start()
        ci_copy(p, c).start()

    def stage_x(p, c):
        x_copy(p, c).wait_recv()
        cj_copy(p, c).start()

    def multiply(p, c):
        ci_copy(p, c).wait_recv()
        cj_copy(p, c).wait_recv()
        if c == CHUNKS:
            return
        if c == 0 and p == 0:
            loads[0].wait()
            loads[1].wait()
        block = rows_all[p, :, :, :, :, span(c)].reshape(total, cols)
        for k in range(local):
            for i, w in enumerate((wg, wu)):
                product = jnp.dot(block, w[k, span(c), :], preferred_element_type=F32)
                if c == 0:
                    acc[k, i] = product
                else:
                    acc[k, i] = acc[k, i] + product

    def activate(p):
        weights = gate_all[p].reshape(total, 128)
        lanes_all = lax.broadcasted_iota(jnp.int32, (total, 128), 1)
        for k in range(local):
            expert = local * (me // SHARDS) + k
            weight = jnp.sum(jnp.where(lanes_all == expert, weights, 0.0), axis=1, keepdims=True)
            value = acc[k, 0]
            value = value / (1.0 + jnp.exp(-value)) * acc[k, 1]
            hid[:, k * hidden : (k + 1) * hidden] = jnp.where(
                weight != 0.0, value * weight, 0.0
            ).astype(BF16)

    def r1_copy(p, c):
        return remote(
            part.at[p, 1 - core, :, :, :, span(c)], recv_core.at[p, :, :, :, span(c)],
            r1_ss.at[p, c], r1_rs.at[p, c], {"expert": twin},
        )

    def r2_copy(p, c):
        return remote(
            send_x.at[p, :, :, span(c)], recv_x.at[p, :, :, span(c)],
            r2_ss.at[p, c], r2_rs.at[p, c], {"expert": across},
        )

    def r3_copy(p, c, step):
        return remote(
            send_a.at[p, step - 1, :, span(c)], recv_a.at[p, step - 1, :, span(c)],
            r3_ss.at[p, c, step - 1], r3_rs.at[p, c, step - 1], {"expert": at_column(step)},
        )

    tile = 256

    def down(p, c):
        if c == 0 and p == 0:
            loads[2].wait()

        @pl.loop(0, cols // tile)
        def _(j):
            at = pl.ds(pl.multiple_of(c * cols + j * tile, tile), tile)
            product = jnp.dot(hid[...], wd[:, at], preferred_element_type=F32)
            part[p, :, :, :, :, at] = product.reshape(2, 2, outer, rows, tile).astype(BF16)

        r1_copy(p, c).start()

    def add_core(p, c):
        r1_copy(p, c).wait_recv()
        for i in range(outer):
            send_x[p, i, :, span(c)] = (
                part[p, core, 1 - b, i, :, span(c)].astype(F32)
                + recv_core[p, 1 - b, i, :, span(c)].astype(F32)
            ).astype(BF16)
        r2_copy(p, c).start()

    def column_sum(p, c, i):
        return (
            part[p, core, b, i, :, span(c)].astype(F32)
            + recv_core[p, b, i, :, span(c)].astype(F32)
            + recv_x[p, i, :, span(c)].astype(F32)
        )

    def add_x(p, c):
        r2_copy(p, c).wait_recv()
        for step in range(1, outer):
            send_a[p, step - 1, :, span(c)] = column_sum(p, c, column(step)).astype(BF16)
            r3_copy(p, c, step).start()

    def finish(p, c):
        result = column_sum(p, c, a)
        for step in range(1, outer):
            r3_copy(p, c, step).wait_recv()
            result = result + recv_a[p, step - 1, :, span(c)].astype(F32)
        out_ref[p, :, span(c)] = (hbuf[p, :, span(c)].astype(F32) + result).astype(BF16)

        @pl.when(section < sections - 1)
        def _():
            h_copy(p, c).start()

    everything = CHUNKS + 1

    @pl.when(section == 0)
    def _():
        for p in range(PARTS):
            send_rows(p, False)

    @pl.when(section > 0)
    def _():
        send_rows(0, True)

    def due(t, lag, count):
        return lag <= t < lag + count

    for p in range(PARTS + 1):
        steps = max(everything + GATHER_LAGS[-1], CHUNKS + REDUCE_LAGS[-1])
        for t in range(steps):
            if p > 0 and due(t, 0, CHUNKS):
                down(p - 1, t)
            if p < PARTS and due(t, 0, everything):
                stage_a(p, t)
            if p > 0 and due(t, REDUCE_LAGS[0], CHUNKS):
                add_core(p - 1, t - REDUCE_LAGS[0])
            if p < PARTS and due(t, GATHER_LAGS[0], everything):
                stage_x(p, t - GATHER_LAGS[0])
            if p > 0 and due(t, REDUCE_LAGS[1], CHUNKS):
                add_x(p - 1, t - REDUCE_LAGS[1])
            if p + 1 < PARTS and t == everything:

                @pl.when(section > 0)
                def _():
                    send_rows(p + 1, True)

            if p < PARTS and due(t, GATHER_LAGS[1], everything):
                multiply(p, t - GATHER_LAGS[1])
            if p > 0 and due(t, REDUCE_LAGS[2], CHUNKS):
                finish(p - 1, t - REDUCE_LAGS[2])
        if p < PARTS:
            activate(p)

    for p in range(PARTS):
        for c in range(everything):
            for step in range(1, outer):
                a_copy(p, c, step).wait_send()
            x_copy(p, c).wait_send()
            ci_copy(p, c).wait_send()
            cj_copy(p, c).wait_send()
        for c in range(CHUNKS):
            r1_copy(p, c).wait_send()
            r2_copy(p, c).wait_send()
            for step in range(1, outer):
                r3_copy(p, c, step).wait_send()

    @pl.when(section < sections - 1)
    def _():
        for p in range(PARTS):
            for c in range(CHUNKS):
                h_copy(p, c).wait_send()


def shards(x_in, gains, router, w_gate, w_up, w_down, route_ids, stopped):
    batches, per, width = x_in.shape
    rows = batches * per // PARTS
    local, _, hidden = w_gate.shape[2:]
    experts = router.shape[2]
    picks = route_ids.shape[3]
    outer = lax.axis_size("expert") // 4
    dma = lambda *shape: pltpu.SemaphoreType.DMA(shape)
    vmem = pl.BlockSpec(memory_space=pltpu.VMEM)
    anywhere = pl.BlockSpec(memory_space=pl.ANY)
    total = 4 * outer * rows
    more = CHUNKS + 1
    result = pl.pallas_call(
        relay_kernel,
        out_shape=jax.ShapeDtypeStruct((PARTS, rows, width), BF16),
        in_specs=[vmem] * 5 + [anywhere] * 3,
        out_specs=vmem,
        scratch_shapes=[
            pltpu.VMEM((PARTS, rows, width), BF16),
            pltpu.VMEM((local, width, hidden), BF16),
            pltpu.VMEM((local, width, hidden), BF16),
            pltpu.VMEM((local * hidden, width), BF16),
            pltpu.VMEM((PARTS, 2, 2, outer, rows, width), BF16),
            pltpu.VMEM((PARTS, 2, 2, outer, rows, 128), F32),
            pltpu.VMEM((local, 2, total, hidden), F32),
            pltpu.VMEM((total, local * hidden), BF16),
            pltpu.VMEM((PARTS, 2, 2, outer, rows, width), BF16),
            pltpu.VMEM((PARTS, 2, outer, rows, width), BF16),
            pltpu.VMEM((PARTS, outer, rows, width), BF16),
            pltpu.VMEM((PARTS, outer, rows, width), BF16),
            pltpu.VMEM((PARTS, outer - 1, rows, width), BF16),
            pltpu.VMEM((PARTS, outer - 1, rows, width), BF16),
            dma(3),
            dma(PARTS, more, outer - 1), dma(PARTS, more, outer - 1),
            dma(PARTS, more), dma(PARTS, more), dma(PARTS, more), dma(PARTS, more), dma(PARTS, more), dma(PARTS, more),
            dma(PARTS, CHUNKS), dma(PARTS, CHUNKS), dma(PARTS, CHUNKS), dma(PARTS, CHUNKS),
            dma(PARTS, CHUNKS, outer - 1), dma(PARTS, CHUNKS, outer - 1),
            dma(PARTS, CHUNKS), dma(PARTS, CHUNKS),
        ],
        compiler_params=pltpu.CompilerParams(
            collective_id=0, has_side_effects=True, vmem_limit_bytes=66 * 1000 * 1000
        ),
    )(
        x_in.reshape(PARTS, rows, width),
        gains,
        jnp.transpose(router[0]),
        route_ids.reshape(PARTS, rows, picks),
        stopped.reshape(PARTS, rows, 1),
        w_gate[0, 0],
        w_up[0, 0],
        w_down.reshape(local * hidden, width),
    )
    return result.reshape(1, batches, per, width)


def solution(mesh):
    in_specs = (
        P(None, "expert", None),
        P("section", None),
        P("section", None, None),
        P("section", "expert", None, None, None),
        P("section", "expert", None, None, None),
        P("section", "expert", None, None, None),
        P("section", None, "expert", None),
        P(None, "expert"),
    )
    out_specs = P("section", None, "expert", None)
    return jax.shard_map(shards, mesh=mesh, in_specs=in_specs, out_specs=out_specs, check_vma=False)
```
